128 devices in a mesh: ha: 16 (over z, y_lo, core), wa: 8 (over x, y_hi).
Axes of the slice: x: 4, y: 4 (y_hi: 2, y_lo: 2; y = y_hi * 2 + y_lo), z: 4, core: 2. Of those that a mesh axis runs over, the one named last changes fastest.
Arguments:
- tokens: bfloat16 [256, 256, 512], P('ha', 'wa'), may hold values from -40 to 40
- cotangent: bfloat16 [256, 256, 512], P('ha', 'wa'), may hold values from -6 to 6
- norm_gain: float32 [512], replicated, may hold values from 0.1 to 1.9
- in_weight: bfloat16 [512, 1536], replicated, may hold values from -0.25 to 0.25
- out_weight: bfloat16 [512, 512], replicated, may hold values from -0.25 to 0.25
- bias_table: float32 [16, 31, 31], replicated, may hold values from -256 to 256
Outputs:
- grad_input: bfloat16 [256, 256, 512], P('ha', 'wa')
- grad_table: float32 [16, 31, 31], replicated
The draws below stay inside these ranges and needn't reach their ends.
All inputs are finite; a program needn't handle non-finite values.
Results may differ from the reference program's by a relative error of at most 0.011.
Values may be sent and summed in bfloat16 or wider, within the bound.
No kernel may reach another device: no remote copies, remote signals or barrier semaphores. Data moves between devices by JAX's collectives and lax.ppermute only.
A program may use at most 128 MiB of HBM per device.

```python
import jax
import jax.numpy as jnp
from jax import lax

D = 512
HEADS = 16
HEAD_DIM = 32
WIN = 16
TAB = 31
HI = 256
WI = 256


def draw_tokens(key, part):
    key_noise = jax.random.fold_in(key, 11)
    base_draw = jax.random.normal(key_noise, (HI, WI, D), jnp.float32)
    return jnp.clip(base_draw, -40.0, 40.0).astype(jnp.bfloat16)


def draw_bias_table(key, part):
    key_noise = jax.random.fold_in(key, 21)
    base_draw = jax.random.normal(key_noise, (HEADS, TAB, TAB), jnp.float32)
    return jnp.clip(base_draw, -256.0, 256.0)


def steps_of(own_key, dims, pieces, least, largest):
    gain = 1.0
    for axis_at, shards_of in pieces:
        heights = jax.random.uniform(jax.random.fold_in(jax.random.fold_in(own_key, 6), axis_at), (shards_of,), jnp.float32, least / len(pieces), largest / len(pieces))
        gain = gain * jnp.repeat(jnp.exp(heights), dims[axis_at] // shards_of).reshape((-1,) + (1,) * (len(dims) - 1 - axis_at))
    return gain


def scatter_about(rng, dims, width, reach, cuts=(), dtype=jnp.bfloat16):
    values = jax.random.normal(rng, dims, jnp.float32) * width
    if len(cuts) > 0:
        values = steps_of(rng, dims, cuts, -0.22, 0.18) * values
    return jnp.clip(values, min=-reach, max=reach).astype(dtype)


def setup_inputs(seed: int = 0) -> dict:
    seeds = jax.random.split(jax.random.key(seed), 7)
    return {
        "tokens": draw_tokens(jax.random.fold_in(seeds[6], 71), 0),
        "cotangent": scatter_about(seeds[1], (HI, WI, D), 1.0, 6.0, ((0, 16), (1, 8))),
        "norm_gain": jnp.clip(1.0 + 0.18 * jax.random.normal(seeds[2], (D,), jnp.float32), 0.1, 1.9),
        "in_weight": scatter_about(seeds[3], (D, 3 * D), D ** -0.5, 0.25),
        "out_weight": scatter_about(seeds[4], (D, D), D ** -0.5, 0.25),
        "bias_table": draw_bias_table(jax.random.fold_in(seeds[6], 71), 0),
    }


NORM_EPS = 1e-05

def offset_hot():
    places = jnp.arange(WIN)
    slot_ids = jnp.arange(TAB)
    return (places[:, None, None] - places[None, :, None] + (WIN - 1) == slot_ids[None, None, :]).astype(jnp.float32)

def full_bias(bias_table, offset_table):
    partial_rows = jnp.einsum('abd,hde->habe', offset_table, bias_table, precision=lax.Precision.HIGHEST)
    spread = jnp.einsum('uve,habe->haubv', offset_table, partial_rows, precision=lax.Precision.HIGHEST)
    return spread.reshape(HEADS, WIN * WIN, WIN * WIN)

def group_grad(group_tokens, group_cot, norm_gain, in_weight, out_weight, bias_full, offset_table):
    group_rows = WIN * WIN
    tokens_wide = group_tokens.astype(jnp.float32)
    center = lax.optimization_barrier(jnp.mean(tokens_wide, axis=-1, keepdims=True))
    shifted = tokens_wide - center
    inv_std = lax.rsqrt(lax.optimization_barrier(jnp.mean(shifted * shifted, axis=-1, keepdims=True)) + NORM_EPS)
    unit_rows = shifted * inv_std
    normed = (unit_rows * norm_gain).astype(jnp.bfloat16)
    mixed_rows = jnp.dot(normed, in_weight, preferred_element_type=jnp.float32)
    query_scale = HEAD_DIM ** (-0.5)
    queries = (mixed_rows[:, :D] * query_scale).astype(jnp.bfloat16).reshape(group_rows, HEADS, HEAD_DIM)
    key_rows = mixed_rows[:, D:2 * D].astype(jnp.bfloat16).reshape(group_rows, HEADS, HEAD_DIM)
    values = mixed_rows[:, 2 * D:].astype(jnp.bfloat16).reshape(group_rows, HEADS, HEAD_DIM)
    scores = jnp.einsum('thd,shd->hts', queries.astype(jnp.float32), key_rows.astype(jnp.float32)) + bias_full
    row_top = lax.optimization_barrier(jnp.max(scores, axis=-1, keepdims=True))
    exponent = jnp.exp(scores - row_top)
    attn_probs = exponent / lax.optimization_barrier(jnp.sum(exponent, axis=-1, keepdims=True))
    probs_half = attn_probs.astype(jnp.bfloat16)
    grad_out = lax.dot_general(group_cot, out_weight, (((1,), (1,)), ((), ())), preferred_element_type=jnp.float32)
    grad_out = grad_out.astype(jnp.bfloat16).reshape(group_rows, HEADS, HEAD_DIM)
    grad_probs = jnp.einsum('thd,shd->hts', grad_out.astype(jnp.float32), values.astype(jnp.float32))
    grad_values = jnp.einsum('hts,thd->shd', probs_half.astype(jnp.float32), grad_out.astype(jnp.float32)).astype(jnp.bfloat16)
    grad_scores = attn_probs * (grad_probs - lax.optimization_barrier(jnp.sum(attn_probs * grad_probs, axis=-1, keepdims=True)))
    scores_half = grad_scores.astype(jnp.bfloat16).astype(jnp.float32)
    grad_queries = (jnp.einsum('hts,shd->thd', scores_half, key_rows.astype(jnp.float32)) * query_scale).astype(jnp.bfloat16)
    grad_keys = jnp.einsum('hts,thd->shd', scores_half, queries.astype(jnp.float32)).astype(jnp.bfloat16)
    grad_mixed = jnp.concatenate([grad_queries.reshape(group_rows, D), grad_keys.reshape(group_rows, D), grad_values.reshape(group_rows, D)], axis=1)
    grad_normed = lax.dot_general(grad_mixed, in_weight, (((1,), (1,)), ((), ())), preferred_element_type=jnp.float32)
    grad_unit = grad_normed * norm_gain
    grad_rows = inv_std * (grad_unit - lax.optimization_barrier(jnp.mean(grad_unit, axis=-1, keepdims=True)) - unit_rows * lax.optimization_barrier(jnp.mean(grad_unit * unit_rows, axis=-1, keepdims=True)))
    folded = jnp.einsum('haubv,uve->habe', grad_scores.reshape(HEADS, WIN, WIN, WIN, WIN), offset_table, precision=lax.Precision.HIGHEST)
    table_part = jnp.einsum('habe,abd->hde', folded, offset_table, precision=lax.Precision.HIGHEST)
    return (grad_rows.astype(jnp.bfloat16), table_part)

def reference(tokens, cotangent, norm_gain, in_weight, out_weight, bias_table):
    stride_h = HI // WIN
    stride_w = WI // WIN
    offset_table = offset_hot()
    bias_full = full_bias(bias_table, offset_table)

    def regroup(field):
        return field.reshape(WIN, stride_h, WIN, stride_w, D).transpose(1, 3, 0, 2, 4).reshape(stride_h * stride_w, WIN * WIN, D)

    def group_step(table_total, pair_rows):
        grad_rows, table_part = group_grad(pair_rows[0], pair_rows[1], norm_gain, in_weight, out_weight, bias_full, offset_table)
        return (table_total + table_part, grad_rows)
    table_total, grad_groups = lax.scan(group_step, jnp.zeros((HEADS, TAB, TAB), jnp.float32), (regroup(tokens), regroup(cotangent)))
    grad_input = grad_groups.reshape(stride_h, stride_w, WIN, WIN, D).transpose(2, 0, 3, 1, 4).reshape(HI, WI, D)
    return (grad_input, table_total)
```

```python
import jax
import jax.numpy as jnp
from jax import lax
from jax.experimental import pallas as pl
from jax.experimental.pallas import tpu as pltpu
from jax.sharding import PartitionSpec as P

D = 512
HEADS = 16
HEAD_DIM = 32
WIN = 16
TAB = 31
NORM_EPS = 1e-05
AXES = ("ha", "wa")
BF16 = jnp.bfloat16
F32 = jnp.float32


def iota(shape, dim):
    return lax.broadcasted_iota(jnp.int32, shape, dim)


def bits(x, low, count):
    return lax.bitwise_and(lax.shift_right_logical(x, low), (1 << count) - 1)


def one_hot(source):
    o = iota((256, 256), 0)
    return jnp.where(source(o) == iota((256, 256), 1), 1.0, 0.0).astype(BF16)


def move_rows(matrix, rows):
    return jnp.dot(matrix, rows, preferred_element_type=F32).astype(BF16)


def pack_kernel(tok_ref, cot_ref, out_ref):
    perm = one_hot(
        lambda o: bits(o, 2, 1) * 128
        + bits(o, 6, 2) * 32
        + bits(o, 0, 1) * 16
        + bits(o, 3, 3) * 2
        + bits(o, 1, 1)
    )
    for q in range(4):
        rows = jnp.concatenate(
            [
                tok_ref[4 * q : 4 * q + 4].reshape(128, D),
                cot_ref[4 * q : 4 * q + 4].reshape(128, D),
            ],
            axis=0,
        )
        out_ref[256 * q : 256 * q + 256, :] = move_rows(perm, rows)


def unpack_kernel(in_ref, out_ref):
    perm = one_hot(
        lambda o: bits(o, 5, 2) * 64
        + bits(o, 1, 3) * 8
        + bits(o, 7, 1) * 4
        + bits(o, 0, 1) * 2
        + bits(o, 4, 1)
    )
    for q in range(4):
        rows = move_rows(perm, in_ref[256 * q : 256 * q + 256, :])
        out_ref[4 * q : 4 * q + 4, :, 0:256] = rows[0:128].reshape(4, 32, 256)
        out_ref[4 * q : 4 * q + 4, :, 256:512] = rows[128:256].reshape(4, 32, 256)


def dot_nt(a, b):
    return lax.dot_general(a, b, (((1,), (1,)), ((), ())), preferred_element_type=F32)


def dot_nn(a, b):
    return jnp.dot(a, b, preferred_element_type=F32)


def group_kernel(
    recv_ref, gain_ref, win_ref, wout_ref, pb_ref, nb_ref,
    out_ref, pn_ref,
    unit_ref, inv_ref, q_ref, k_ref, v_ref, go_ref, qt_ref, kt_ref, got_ref,
    dqt_ref, dk_ref, dv_ref, tok_ref, cot_ref,
):
    scale = HEAD_DIM ** (-0.5)
    take = one_hot(
        lambda o: bits(o, 1, 5) * 8 + bits(o, 7, 1) * 4 + bits(o, 6, 1) * 2 + bits(o, 0, 1)
    )
    for q in range(4):
        rows = move_rows(take, recv_ref[256 * q : 256 * q + 256, :])
        for g in range(2):
            at = 256 * g + 64 * q
            tok_ref[at : at + 64, :] = rows[64 * g : 64 * g + 64]
            cot_ref[at : at + 64, :] = rows[128 + 64 * g : 192 + 64 * g]

    for g in range(2):
        sl = slice(256 * g, 256 * g + 256)
        x = tok_ref[sl, :].astype(F32)
        shifted = x - jnp.mean(x, axis=-1, keepdims=True)
        inv_std = lax.rsqrt(jnp.mean(shifted * shifted, axis=-1, keepdims=True) + NORM_EPS)
        unit = shifted * inv_std
        unit_ref[sl, :] = unit
        inv_ref[sl, :] = jnp.broadcast_to(inv_std, (256, 128))
        normed = (unit * gain_ref[...]).astype(BF16)
        qv = dot_nn(normed, win_ref[:, 0:D]) * scale
        q_ref[sl, :] = qv.astype(BF16)
        qt_ref[D * g : D * g + D, :] = qv.T.astype(BF16)
        kv = dot_nn(normed, win_ref[:, D : 2 * D])
        k_ref[sl, :] = kv.astype(BF16)
        kt_ref[D * g : D * g + D, :] = kv.T.astype(BF16)
        v_ref[sl, :] = dot_nn(normed, win_ref[:, 2 * D : 3 * D]).astype(BF16)
        go = dot_nt(cot_ref[sl, :], wout_ref[...])
        go_ref[sl, :] = go.astype(BF16)
        got_ref[D * g : D * g + D, :] = go.T.astype(BF16)

    row = iota((16, 512), 0)
    lane_in = bits(iota((16, 512), 1), 0, 4)
    ahead = (lane_in + row) < 16

    def head(h, carry):
        hb = lax.shift_right_logical(h, 2)
        hh = lax.bitwise_and(h, 3)
        base = pl.multiple_of(hb * 128, 128)
        mine = lax.shift_right_logical(iota((256, 128), 1), 5) == hh

        line = jnp.where(ahead, pb_ref[pl.ds(h, 1), :], nb_ref[pl.ds(h, 1), :])
        for b in (1, 2, 4, 8):
            line = jnp.where(lax.bitwise_and(row, b) != 0, pltpu.roll(line, b, 1), line)
        turned = [line if r == 0 else pltpu.roll(line, 512 - 16 * r, 1) for r in range(8)]
        bias = jnp.concatenate(
            [
                turned[(15 - i) % 8][:, 128 * ((15 - i) // 8) : 128 * ((15 - i) // 8) + 256]
                for i in range(16)
            ],
            axis=0,
        )
        total = None
        for g in range(2):
            sl = slice(256 * g, 256 * g + 256)
            lanes = pl.ds(base, 128)
            zero = jnp.zeros((256, 128), BF16)
            k_mine = jnp.where(mine, k_ref[sl, lanes], zero)
            v_mine = jnp.where(mine, v_ref[sl, lanes], zero)
            q_mine = jnp.where(mine, q_ref[sl, lanes], zero)
            go_mine = jnp.where(mine, go_ref[sl, lanes], zero)
            tall = pl.ds(pl.multiple_of(D * g + hb * 128, 128), 128)
            thin = pl.ds(pl.multiple_of(D * g + h * 32, 32), 32)
            scores = dot_nn(k_mine, qt_ref[tall, :]) + bias
            top = jnp.max(scores, axis=0, keepdims=True)
            exponent = jnp.exp(scores - top)
            probs = exponent * (1.0 / jnp.sum(exponent, axis=0, keepdims=True))
            grad_probs = dot_nn(v_mine, got_ref[tall, :])
            grad_v = dot_nn(probs.astype(BF16), go_mine)
            dv_ref[sl, lanes] = jnp.where(mine, grad_v.astype(BF16), dv_ref[sl, lanes])
            delta = jnp.sum(probs * grad_probs, axis=0, keepdims=True)
            grad_scores = probs * (grad_probs - delta)
            half = grad_scores.astype(BF16)
            grad_k = dot_nn(half, q_mine)
            dk_ref[sl, lanes] = jnp.where(mine, grad_k.astype(BF16), dk_ref[sl, lanes])
            dqt_ref[thin, :] = dot_nn(kt_ref[thin, :], half) * scale
            total = grad_scores if total is None else total + grad_scores

        fold = None
        blank = jnp.zeros((16, 128), F32)
        for r in range(8):
            a = total[16 * (15 - r) : 16 * (15 - r) + 16]
            b = total[16 * (7 - r) : 16 * (7 - r) + 16]
            wide = jnp.concatenate(
                [a[:, 0:128], a[:, 128:256] + b[:, 0:128], b[:, 128:256], blank], axis=1
            )
            if r:
                wide = pltpu.roll(wide, 16 * r, 1)
            fold = wide if fold is None else fold + wide
        for b in (1, 2, 4, 8):
            fold = jnp.where(lax.bitwise_and(row, b) != 0, pltpu.roll(fold, 512 - b, 1), fold)
        near = jnp.where(ahead, fold, 0.0)
        pn_ref[pl.ds(h, 1), 0:512] = jnp.sum(near, axis=0, keepdims=True)
        pn_ref[pl.ds(h, 1), 512:1024] = jnp.sum(fold - near, axis=0, keepdims=True)
        return carry

    lax.fori_loop(0, HEADS, head, 0)

    for g in range(2):
        sl = slice(256 * g, 256 * g + 256)
        grad_q = dqt_ref[D * g : D * g + D, :].T.astype(BF16)
        grad_normed = (
            dot_nt(grad_q, win_ref[:, 0:D])
            + dot_nt(dk_ref[sl, :], win_ref[:, D : 2 * D])
            + dot_nt(dv_ref[sl, :], win_ref[:, 2 * D : 3 * D])
        )
        grad_unit = grad_normed * gain_ref[...]
        unit = unit_ref[sl, :]
        grad_rows = inv_ref[sl, 0:1] * (
            grad_unit
            - jnp.mean(grad_unit, axis=-1, keepdims=True)
            - unit * jnp.mean(grad_unit * unit, axis=-1, keepdims=True)
        )
        tok_ref[sl, :] = grad_rows.astype(BF16)

    give = one_hot(
        lambda o: bits(o, 1, 1) * 128 + bits(o, 2, 1) * 64 + bits(o, 3, 5) * 2 + bits(o, 0, 1)
    )
    for q in range(4):
        rows = jnp.concatenate(
            [
                tok_ref[256 * g + 64 * q : 256 * g + 64 * q + 64, 256 * half : 256 * half + 256]
                for g in range(2)
                for half in range(2)
            ],
            axis=0,
        )
        out_ref[256 * q : 256 * q + 256, :] = move_rows(give, rows)


def device_index(z, y, x, core):
    return (z * 4 + (y % 2) * 2 + core) * 8 + x * 2 + y // 2


def shift_pairs(axis, step):
    pairs = []
    for z in range(4):
        for y in range(4):
            for x in range(4):
                for core in range(2):
                    there = {"z": z, "y": y, "x": x}
                    there[axis] = (there[axis] + step) % 4
                    pairs.append(
                        (
                            device_index(z, y, x, core),
                            device_index(there["z"], there["y"], there["x"], core),
                        )
                    )
    return pairs


def other_core_pairs():
    return [(i, i ^ 8) for i in range(128)]


def sum_everywhere(part):
    core = lax.rem(lax.axis_index("ha"), 2)
    own = lax.dynamic_slice(part, (8 * core, 0), (8, 1024))
    given = lax.dynamic_slice(part, (8 * (1 - core), 0), (8, 1024))
    own = own + lax.ppermute(given, AXES, other_core_pairs())
    for axis in ("z", "x", "y"):
        one, two, three = (lax.ppermute(own, AXES, shift_pairs(axis, s)) for s in (1, 2, 3))
        own = (own + two) + (one + three)
    other = lax.ppermute(own, AXES, other_core_pairs())
    low = jnp.where(core == 0, own, other)
    high = jnp.where(core == 0, other, own)
    return jnp.concatenate([low, high], axis=0)


def split_bias(bias_table):
    zero = jnp.zeros((HEADS, 1, 16), F32)
    near = jnp.concatenate([bias_table[:, :, 15:31], zero], axis=1)
    far = jnp.pad(bias_table[:, :, 0:15], ((0, 0), (0, 0), (1, 0)))
    far = jnp.concatenate([far[:, 1:31], zero, far[:, 0:1]], axis=1)
    return near.reshape(HEADS, 512), far.reshape(HEADS, 512)


def join_table(part):
    near = part[:, 0:512].reshape(HEADS, 32, 16)[:, 0:31]
    far = part[:, 512:1024].reshape(HEADS, 32, 16)
    far = jnp.concatenate([far[:, 31:32], far[:, 0:30]], axis=1)[:, :, 1:16]
    return jnp.concatenate([far, near], axis=2)


def vmem_specs(count):
    return [pl.BlockSpec(memory_space=pltpu.VMEM)] * count


def body(tokens, cotangent, norm_gain, in_weight, out_weight, bias_table):
    sent = pl.pallas_call(
        pack_kernel,
        out_shape=jax.ShapeDtypeStruct((1024, D), BF16),
        in_specs=vmem_specs(2),
        out_specs=vmem_specs(1)[0],
    )(tokens, cotangent)
    near, far = split_bias(bias_table)
    got = lax.all_to_all(sent.reshape(128, 8, D), AXES, split_axis=0, concat_axis=0, tiled=True)
    back, part = pl.pallas_call(
        group_kernel,
        out_shape=(
            jax.ShapeDtypeStruct((1024, 256), BF16),
            jax.ShapeDtypeStruct((HEADS, 1024), F32),
        ),
        in_specs=vmem_specs(6),
        out_specs=tuple(vmem_specs(2)),
        scratch_shapes=[
            pltpu.VMEM((512, D), F32),
            pltpu.VMEM((512, 128), F32),
            pltpu.VMEM((512, D), BF16),
            pltpu.VMEM((512, D), BF16),
            pltpu.VMEM((512, D), BF16),
            pltpu.VMEM((512, D), BF16),
            pltpu.VMEM((2 * D, 256), BF16),
            pltpu.VMEM((2 * D, 256), BF16),
            pltpu.VMEM((2 * D, 256), BF16),
            pltpu.VMEM((2 * D, 256), F32),
            pltpu.VMEM((512, D), BF16),
            pltpu.VMEM((512, D), BF16),
            pltpu.VMEM((512, D), BF16),
            pltpu.VMEM((512, D), BF16),
        ],
        cost_estimate=pl.CostEstimate(
            flops=20_000_000_000, bytes_accessed=8_000_000, transcendentals=2_000_000
        ),
    )(got.reshape(1024, D), norm_gain.reshape(1, D), in_weight, out_weight, near, far)
    returned = lax.all_to_all(
        back.reshape(128, 8, 256), AXES, split_axis=0, concat_axis=0, tiled=True
    )
    table = join_table(sum_everywhere(part))
    grad_input = pl.pallas_call(
        unpack_kernel,
        out_shape=jax.ShapeDtypeStruct((16, 32, D), BF16),
        in_specs=vmem_specs(1),
        out_specs=vmem_specs(1)[0],
    )(returned.reshape(1024, 256))
    return (grad_input, table)


def solution(mesh):
    in_specs = (P("ha", "wa", None), P("ha", "wa", None), P(), P(), P(), P())
    out_specs = (P("ha", "wa", None), P())
    return jax.shard_map(body, mesh=mesh, in_specs=in_specs, out_specs=out_specs, check_vma=False)
```

```python
import jax
import jax.numpy as jnp
from jax import lax
from jax.experimental import pallas as pl
from jax.experimental.pallas import tpu as pltpu
from jax.sharding import PartitionSpec as P

D = 512
HEADS = 16
HEAD_DIM = 32
NORM_EPS = 1e-05
AXES = ("ha", "wa")
BF16 = jnp.bfloat16
F32 = jnp.float32
SMALL_GRANT = 12 << 20
LARGE_GRANT = 50 << 20


def iota(shape, dim):
    return lax.broadcasted_iota(jnp.int32, shape, dim)


def bits(x, low, count):
    return lax.bitwise_and(lax.shift_right_logical(x, low), (1 << count) - 1)


def one_hot(source):
    o = iota((256, 256), 0)
    return jnp.where(source(o) == iota((256, 256), 1), 1.0, 0.0).astype(BF16)


def move_rows(matrix, rows):
    return jnp.dot(matrix, rows, preferred_element_type=F32).astype(BF16)


def pack_kernel(tok_hbm, cot_hbm, out_hbm, rows_in, rows_out, in_sem, out_sem):
    def fetch(q, kind):
        source = (tok_hbm, cot_hbm)[kind]
        return pltpu.make_async_copy(
            source.at[pl.ds(4 * q, 4)], rows_in.at[q, kind], in_sem.at[q, kind]
        )

    def emit(q):
        return pltpu.make_async_copy(
            rows_out.at[pl.ds(256 * q, 256)], out_hbm.at[pl.ds(256 * q, 256)], out_sem.at[q]
        )

    for q in range(4):
        fetch(q, 0).start()
        fetch(q, 1).start()
    perm = one_hot(
        lambda o: bits(o, 2, 1) * 128
        + bits(o, 6, 2) * 32
        + bits(o, 0, 1) * 16
        + bits(o, 3, 3) * 2
        + bits(o, 1, 1)
    )
    for q in range(4):
        fetch(q, 0).wait()
        fetch(q, 1).wait()
        rows_out[256 * q : 256 * q + 256, :] = move_rows(perm, rows_in[q].reshape(256, D))
        emit(q).start()
    for q in range(4):
        emit(q).wait()


def unpack_kernel(in_ref, out_ref):
    perm = one_hot(
        lambda o: bits(o, 5, 2) * 64
        + bits(o, 1, 3) * 8
        + bits(o, 7, 1) * 4
        + bits(o, 0, 1) * 2
        + bits(o, 4, 1)
    )
    for q in range(4):
        rows = move_rows(perm, in_ref[256 * q : 256 * q + 256, :])
        out_ref[4 * q : 4 * q + 4, :, 0:256] = rows[0:128].reshape(4, 32, 256)
        out_ref[4 * q : 4 * q + 4, :, 256:512] = rows[128:256].reshape(4, 32, 256)


def dot_nn(a, b):
    return jnp.dot(a, b, preferred_element_type=F32)


def prep_kernel(near_ref, far_ref, win_ref, wout_ref, bias_ref, win_t_ref, wout_t_ref):
    row = iota((16, 512), 0)
    ahead = (bits(iota((16, 512), 1), 0, 4) + row) < 16

    def head(h, carry):
        line = jnp.where(ahead, near_ref[pl.ds(h, 1), :], far_ref[pl.ds(h, 1), :])
        for b in (1, 2, 4, 8):
            line = jnp.where(lax.bitwise_and(row, b) != 0, pltpu.roll(line, b, 1), line)
        for r in range(8):
            turned = line if r == 0 else pltpu.roll(line, 512 - 16 * r, 1)
            bias_ref[h, 16 * (15 - r) : 16 * (15 - r) + 16, :] = turned[:, 0:256]
            bias_ref[h, 16 * (7 - r) : 16 * (7 - r) + 16, :] = turned[:, 128:384]
        return carry

    lax.fori_loop(0, HEADS, head, 0)
    for part in range(3):
        cols = slice(D * part, D * part + D)
        win_t_ref[cols, :] = win_ref[:, cols].astype(F32).T.astype(BF16)
    wout_t_ref[...] = wout_ref[...].astype(F32).T.astype(BF16)


def group_kernel(
    recv_ref, gain_ref, win_ref, win_t_hbm, wout_t_hbm, bias_hbm,
    out_ref, pn_ref,
    unit_ref, inv_ref, q_ref, k_ref, v_ref, go_ref, qt_ref, kt_ref, got_ref,
    dqt_ref, dk_ref, dv_ref, tok_ref, cot_ref, dk_part, dv_part,
    win_t_ref, wout_t_ref, bias_ref, weight_sem, bias_sem,
):
    scale = HEAD_DIM ** (-0.5)
    fetch_out = pltpu.make_async_copy(wout_t_hbm, wout_t_ref, weight_sem.at[0])
    fetch_in = pltpu.make_async_copy(win_t_hbm, win_t_ref, weight_sem.at[1])

    def fetch_bias(hb):
        four = pl.ds(4 * hb, 4)
        return pltpu.make_async_copy(bias_hbm.at[four], bias_ref.at[four], bias_sem.at[hb])

    fetch_out.start()
    for hb in range(4):
        fetch_bias(hb).start()
    fetch_in.start()
    take = one_hot(
        lambda o: bits(o, 1, 5) * 8 + bits(o, 7, 1) * 4 + bits(o, 6, 1) * 2 + bits(o, 0, 1)
    )
    for q in range(4):
        rows = move_rows(take, recv_ref[256 * q : 256 * q + 256, :])
        for g in range(2):
            at = 256 * g + 64 * q
            tok_ref[at : at + 64, :] = rows[64 * g : 64 * g + 64]
            cot_ref[at : at + 64, :] = rows[128 + 64 * g : 192 + 64 * g]

    for g in range(2):
        sl = slice(256 * g, 256 * g + 256)
        x = tok_ref[sl, :].astype(F32)
        shifted = x - jnp.mean(x, axis=-1, keepdims=True)
        inv_std = lax.rsqrt(jnp.mean(shifted * shifted, axis=-1, keepdims=True) + NORM_EPS)
        unit = shifted * inv_std
        unit_ref[sl, :] = unit
        inv_ref[sl, :] = jnp.broadcast_to(inv_std, (256, 128))
        normed = (unit * gain_ref[...]).astype(BF16)
        qv = dot_nn(normed, win_ref[:, 0:D]) * scale
        q_ref[sl, :] = qv.astype(BF16)
        qt_ref[D * g : D * g + D, :] = qv.T.astype(BF16)
        kv = dot_nn(normed, win_ref[:, D : 2 * D])
        k_ref[sl, :] = kv.astype(BF16)
        kt_ref[D * g : D * g + D, :] = kv.T.astype(BF16)
        v_ref[sl, :] = dot_nn(normed, win_ref[:, 2 * D : 3 * D]).astype(BF16)
        if g == 0:
            fetch_out.wait()
        go = dot_nn(cot_ref[sl, :], wout_t_ref[...])
        go_ref[sl, :] = go.astype(BF16)
        got_ref[D * g : D * g + D, :] = go.T.astype(BF16)

    row = iota((16, 512), 0)
    ahead = (bits(iota((16, 512), 1), 0, 4) + row) < 16
    owner = lax.shift_right_logical(iota((256, 128), 1), 5)

    def only(rows, hh):
        pieces = [jnp.zeros((32 * hh, 256), BF16)] if hh else []
        pieces.append(rows)
        if hh < 3:
            pieces.append(jnp.zeros((96 - 32 * hh, 256), BF16))
        return jnp.concatenate(pieces, axis=0)

    def block(hb, carry):
        lanes = pl.ds(pl.multiple_of(hb * 128, 128), 128)
        fetch_bias(hb).wait()

        def thin(g, hh):
            return pl.ds(pl.multiple_of(D * g + hb * 128 + 32 * hh, 32), 32)

        def forward(hh, g):
            sl = slice(256 * g, 256 * g + 256)
            scores = dot_nn(k_ref[sl, lanes], only(qt_ref[thin(g, hh), :], hh))
            grad_probs = dot_nn(v_ref[sl, lanes], only(got_ref[thin(g, hh), :], hh))
            return scores, grad_probs

        def backward(hh, g, scores, grad_probs):
            sl = slice(256 * g, 256 * g + 256)
            probs_half, scores_half, grads = [], [], []
            for t in (slice(0, 128), slice(128, 256)):
                shifted = scores[:, t] + bias_ref[hb * 4 + hh, :, t]
                exponent = jnp.exp(shifted - jnp.max(shifted, axis=0, keepdims=True))
                probs = exponent * (1.0 / jnp.sum(exponent, axis=0, keepdims=True))
                probs_half.append(probs.astype(BF16))
                delta = jnp.sum(probs * grad_probs[:, t], axis=0, keepdims=True)
                grad = probs * (grad_probs[:, t] - delta)
                scores_half.append(grad.astype(BF16))
                grads.append(grad)
            half = jnp.concatenate(scores_half, axis=1)
            mine = owner == hh
            grad_v = dot_nn(jnp.concatenate(probs_half, axis=1), go_ref[sl, lanes])
            pltpu.store(dv_part.at[sl, :], grad_v, mask=mine)
            pltpu.store(dk_part.at[sl, :], dot_nn(half, q_ref[sl, lanes]), mask=mine)
            dqt_ref[thin(g, hh), :] = dot_nn(kt_ref[thin(g, hh), :], half) * scale
            return grads

        units = [(hh, g) for hh in range(4) for g in range(2)]
        ready = forward(*units[0])
        total = None
        for n, (hh, g) in enumerate(units):
            after = forward(*units[n + 1]) if n + 1 < len(units) else None
            grads = backward(hh, g, *ready)
            ready = after
            if g == 0:
                total = grads
                continue
            left, right = total[0] + grads[0], total[1] + grads[1]
            fold = None
            blank = jnp.zeros((16, 128), F32)
            for r in range(8):
                a = slice(16 * (15 - r), 16 * (15 - r) + 16)
                b = slice(16 * (7 - r), 16 * (7 - r) + 16)
                wide = jnp.concatenate([left[a], right[a] + left[b], right[b], blank], axis=1)
                if r:
                    wide = pltpu.roll(wide, 16 * r, 1)
                fold = wide if fold is None else fold + wide
            for b in (1, 2, 4, 8):
                fold = jnp.where(lax.bitwise_and(row, b) != 0, pltpu.roll(fold, 512 - b, 1), fold)
            near = jnp.where(ahead, fold, 0.0)
            h = hb * 4 + hh
            pn_ref[pl.ds(h, 1), 0:512] = jnp.sum(near, axis=0, keepdims=True)
            pn_ref[pl.ds(h, 1), 512:1024] = jnp.sum(fold - near, axis=0, keepdims=True)
        dk_ref[:, lanes] = dk_part[...].astype(BF16)
        dv_ref[:, lanes] = dv_part[...].astype(BF16)
        return carry

    lax.fori_loop(0, 4, block, 0)
    fetch_in.wait()

    for g in range(2):
        sl = slice(256 * g, 256 * g + 256)
        grad_q = dqt_ref[D * g : D * g + D, :].T.astype(BF16)
        grad_normed = (
            dot_nn(grad_q, win_t_ref[0:D, :])
            + dot_nn(dk_ref[sl, :], win_t_ref[D : 2 * D, :])
            + dot_nn(dv_ref[sl, :], win_t_ref[2 * D : 3 * D, :])
        )
        grad_unit = grad_normed * gain_ref[...]
        unit = unit_ref[sl, :]
        grad_rows = inv_ref[sl, 0:1] * (
            grad_unit
            - jnp.mean(grad_unit, axis=-1, keepdims=True)
            - unit * jnp.mean(grad_unit * unit, axis=-1, keepdims=True)
        )
        tok_ref[sl, :] = grad_rows.astype(BF16)

    give = one_hot(
        lambda o: bits(o, 1, 1) * 128 + bits(o, 2, 1) * 64 + bits(o, 3, 5) * 2 + bits(o, 0, 1)
    )
    for q in range(4):
        rows = jnp.concatenate(
            [
                tok_ref[256 * g + 64 * q : 256 * g + 64 * q + 64, 256 * half : 256 * half + 256]
                for g in range(2)
                for half in range(2)
            ],
            axis=0,
        )
        out_ref[256 * q : 256 * q + 256, :] = move_rows(give, rows)


def device_index(z, y, x, core):
    return (z * 4 + (y % 2) * 2 + core) * 8 + x * 2 + y // 2


def shift_pairs(axis, step):
    pairs = []
    for z in range(4):
        for y in range(4):
            for x in range(4):
                for core in range(2):
                    there = {"z": z, "y": y, "x": x}
                    there[axis] = (there[axis] + step) % 4
                    pairs.append(
                        (
                            device_index(z, y, x, core),
                            device_index(there["z"], there["y"], there["x"], core),
                        )
                    )
    return pairs


def other_core_pairs():
    return [(i, i ^ 8) for i in range(128)]


def sum_everywhere(part):
    core = lax.rem(lax.axis_index("ha"), 2)
    own = lax.dynamic_slice(part, (8 * core, 0), (8, 1024))
    given = lax.dynamic_slice(part, (8 * (1 - core), 0), (8, 1024))
    got = lax.ppermute(given, AXES, other_core_pairs())
    own = own + got
    for axis in ("z", "x", "y"):
        one, two, three = (lax.ppermute(own, AXES, shift_pairs(axis, s)) for s in (1, 2, 3))
        own = (own + two) + (one + three)
    other = lax.ppermute(own, AXES, other_core_pairs())
    low = jnp.where(core == 0, own, other)
    high = jnp.where(core == 0, other, own)
    return jnp.concatenate([low, high], axis=0)


def split_bias(bias_table):
    zero = jnp.zeros((HEADS, 1, 16), F32)
    near = jnp.concatenate([bias_table[:, :, 15:31], zero], axis=1)
    far = jnp.pad(bias_table[:, :, 0:15], ((0, 0), (0, 0), (1, 0)))
    far = jnp.concatenate([far[:, 1:31], zero, far[:, 0:1]], axis=1)
    return near.reshape(HEADS, 512), far.reshape(HEADS, 512)


def join_table(part):
    near = part[:, 0:512].reshape(HEADS, 32, 16)[:, 0:31]
    far = part[:, 512:1024].reshape(HEADS, 32, 16)
    far = jnp.concatenate([far[:, 31:32], far[:, 0:30]], axis=1)[:, :, 1:16]
    return jnp.concatenate([far, near], axis=2)


def vmem_specs(count):
    return [pl.BlockSpec(memory_space=pltpu.VMEM)] * count


def step(tokens, cotangent, norm_gain, in_weight, out_weight, bias_table):
    sent = pl.pallas_call(
        pack_kernel,
        out_shape=jax.ShapeDtypeStruct((1024, D), BF16),
        in_specs=[pl.BlockSpec(memory_space=pl.ANY)] * 2,
        out_specs=pl.BlockSpec(memory_space=pl.ANY),
        scratch_shapes=[
            pltpu.VMEM((4, 2, 4, 32, D), BF16),
            pltpu.VMEM((1024, D), BF16),
            pltpu.SemaphoreType.DMA((4, 2)),
            pltpu.SemaphoreType.DMA((4,)),
        ],
    )(tokens, cotangent)
    near, far = split_bias(bias_table)
    got = lax.all_to_all(sent.reshape(128, 8, D), AXES, split_axis=0, concat_axis=0, tiled=True)
    bias, in_turned, out_turned = pl.pallas_call(
        prep_kernel,
        out_shape=(
            jax.ShapeDtypeStruct((HEADS, 256, 256), F32),
            jax.ShapeDtypeStruct((3 * D, D), BF16),
            jax.ShapeDtypeStruct((D, D), BF16),
        ),
        in_specs=vmem_specs(4),
        out_specs=tuple(vmem_specs(3)),
        compiler_params=pltpu.CompilerParams(vmem_limit_bytes=LARGE_GRANT),
    )(near, far, in_weight, out_weight)
    back, part = pl.pallas_call(
        group_kernel,
        out_shape=(
            jax.ShapeDtypeStruct((1024, 256), BF16),
            jax.ShapeDtypeStruct((HEADS, 1024), F32),
        ),
        in_specs=vmem_specs(3) + [pl.BlockSpec(memory_space=pltpu.HBM)] * 3,
        out_specs=tuple(vmem_specs(2)),
        scratch_shapes=[
            pltpu.VMEM((512, D), F32),
            pltpu.VMEM((512, 128), F32),
            pltpu.VMEM((512, D), BF16),
            pltpu.VMEM((512, D), BF16),
            pltpu.VMEM((512, D), BF16),
            pltpu.VMEM((512, D), BF16),
            pltpu.VMEM((2 * D, 256), BF16),
            pltpu.VMEM((2 * D, 256), BF16),
            pltpu.VMEM((2 * D, 256), BF16),
            pltpu.VMEM((2 * D, 256), F32),
            pltpu.VMEM((512, D), BF16),
            pltpu.VMEM((512, D), BF16),
            pltpu.VMEM((512, D), BF16),
            pltpu.VMEM((512, D), BF16),
            pltpu.VMEM((512, 128), F32),
            pltpu.VMEM((512, 128), F32),
            pltpu.VMEM((3 * D, D), BF16),
            pltpu.VMEM((D, D), BF16),
            pltpu.VMEM((HEADS, 256, 256), F32),
            pltpu.SemaphoreType.DMA((2,)),
            pltpu.SemaphoreType.DMA((4,)),
        ],
        compiler_params=pltpu.CompilerParams(vmem_limit_bytes=LARGE_GRANT),
        cost_estimate=pl.CostEstimate(
            flops=20_000_000_000, bytes_accessed=8_000_000, transcendentals=2_000_000
        ),
    )(got.reshape(1024, D), norm_gain.reshape(1, D), in_weight, in_turned, out_turned, bias)
    returned = lax.all_to_all(
        back.reshape(128, 8, 256), AXES, split_axis=0, concat_axis=0, tiled=True
    )
    table = join_table(sum_everywhere(part))
    grad_input = pl.pallas_call(
        unpack_kernel,
        out_shape=jax.ShapeDtypeStruct((16, 32, D), BF16),
        in_specs=vmem_specs(1),
        out_specs=vmem_specs(1)[0],
        compiler_params=pltpu.CompilerParams(vmem_limit_bytes=SMALL_GRANT),
    )(returned.reshape(1024, 256))
    return (grad_input, table)


def solution(mesh):
    in_specs = (P("ha", "wa", None), P("ha", "wa", None), P(), P(), P(), P())
    out_specs = (P("ha", "wa", None), P())
    return jax.shard_map(step, mesh=mesh, in_specs=in_specs, out_specs=out_specs, check_vma=False)
```

```python
import jax
import jax.numpy as jnp
from jax import lax
from jax.experimental import pallas as pl
from jax.experimental.pallas import tpu as pltpu
from jax.sharding import PartitionSpec as P

D = 512
HEADS = 16
HEAD_DIM = 32
NORM_EPS = 1e-05
AXES = ("ha", "wa")
BF16 = jnp.bfloat16
F32 = jnp.float32
SMALL_GRANT = 12 << 20
LARGE_GRANT = 50 << 20
LINE_ROWS = 2048


def iota(shape, dim):
    return lax.broadcasted_iota(jnp.int32, shape, dim)


def bits(x, low, count):
    return lax.bitwise_and(lax.shift_right_logical(x, low), (1 << count) - 1)


def one_hot(source):
    o = iota((256, 256), 0)
    return jnp.where(source(o) == iota((256, 256), 1), 1.0, 0.0).astype(BF16)


def move_rows(matrix, rows):
    return jnp.dot(matrix, rows, preferred_element_type=F32).astype(BF16)


def pack_kernel(tok_hbm, cot_hbm, out_hbm, rows_in, rows_out, in_sem, out_sem):
    def fetch(q, kind):
        source = (tok_hbm, cot_hbm)[kind]
        return pltpu.make_async_copy(
            source.at[pl.ds(4 * q, 4)], rows_in.at[q, kind], in_sem.at[q, kind]
        )

    def emit(q):
        return pltpu.make_async_copy(
            rows_out.at[pl.ds(256 * q, 256)], out_hbm.at[pl.ds(256 * q, 256)], out_sem.at[q]
        )

    for q in range(4):
        fetch(q, 0).start()
        fetch(q, 1).start()
    perm = one_hot(
        lambda o: bits(o, 2, 1) * 128
        + bits(o, 6, 2) * 32
        + bits(o, 0, 1) * 16
        + bits(o, 3, 3) * 2
        + bits(o, 1, 1)
    )
    for q in range(4):
        fetch(q, 0).wait()
        fetch(q, 1).wait()
        rows_out[256 * q : 256 * q + 256, :] = move_rows(perm, rows_in[q].reshape(256, D))
        emit(q).start()
    for q in range(4):
        emit(q).wait()


def unpack_kernel(in_ref, out_ref):
    perm = one_hot(
        lambda o: bits(o, 5, 2) * 64
        + bits(o, 1, 3) * 8
        + bits(o, 7, 1) * 4
        + bits(o, 0, 1) * 2
        + bits(o, 4, 1)
    )
    for q in range(4):
        rows = move_rows(perm, in_ref[256 * q : 256 * q + 256, :])
        out_ref[4 * q : 4 * q + 4, :, 0:256] = rows[0:128].reshape(4, 32, 256)
        out_ref[4 * q : 4 * q + 4, :, 256:512] = rows[128:256].reshape(4, 32, 256)


def dot_nn(a, b):
    return jnp.dot(a, b, preferred_element_type=F32)


def prep_kernel(near_ref, far_ref, win_ref, wout_ref, line_hbm, turned_ref, line_ref, sem):
    row = iota((16, 512), 0)
    ahead = (bits(iota((16, 512), 1), 0, 4) + row) < 16

    def head(h, carry):
        line = jnp.where(ahead, near_ref[pl.ds(h, 1), :], far_ref[pl.ds(h, 1), :])
        for b in (1, 2, 4, 8):
            line = jnp.where(lax.bitwise_and(row, b) != 0, pltpu.roll(line, b, 1), line)
        line_ref[pl.ds(pl.multiple_of(16 * h, 16), 16), :] = line
        return carry

    lax.fori_loop(0, HEADS, head, 0)
    emit = pltpu.make_async_copy(line_ref, line_hbm.at[pl.ds(0, 256)], sem)
    emit.start()
    for part in range(3):
        cols = slice(D * part, D * part + D)
        turned_ref[cols, :] = win_ref[:, cols].astype(F32).T.astype(BF16)
    turned_ref[3 * D : 4 * D, :] = wout_ref[...].astype(F32).T.astype(BF16)
    emit.wait()


def group_kernel(
    recv_ref, gain_ref, win_ref, line_hbm, turned_hbm,
    out_ref, pn_ref,
    unit_ref, inv_ref, q_ref, k_ref, v_ref, go_ref, qt_ref, kt_ref, got_ref,
    dqt_ref, dk_ref, dv_ref, tok_ref, cot_ref, dk_part, dv_part,
    win_t_ref, wout_t_ref, bias_ref, line_ref, weight_sem,
):
    scale = HEAD_DIM ** (-0.5)
    fetch_out = pltpu.make_async_copy(
        turned_hbm.at[pl.ds(3 * D, D)], wout_t_ref, weight_sem.at[0]
    )
    fetch_in = pltpu.make_async_copy(
        turned_hbm.at[pl.ds(0, 3 * D)], win_t_ref, weight_sem.at[1]
    )

    fetch_lines = pltpu.make_async_copy(
        line_hbm.at[pl.ds(0, 256)], line_ref, weight_sem.at[2]
    )
    fetch_out.start()
    fetch_lines.start()
    fetch_in.start()
    take = one_hot(
        lambda o: bits(o, 1, 5) * 8 + bits(o, 7, 1) * 4 + bits(o, 6, 1) * 2 + bits(o, 0, 1)
    )
    for q in range(4):
        rows = move_rows(take, recv_ref[256 * q : 256 * q + 256, :])
        for g in range(2):
            at = 256 * g + 64 * q
            tok_ref[at : at + 64, :] = rows[64 * g : 64 * g + 64]
            cot_ref[at : at + 64, :] = rows[128 + 64 * g : 192 + 64 * g]

    for g in range(2):
        sl = slice(256 * g, 256 * g + 256)
        x = tok_ref[sl, :].astype(F32)
        shifted = x - jnp.mean(x, axis=-1, keepdims=True)
        inv_std = lax.rsqrt(jnp.mean(shifted * shifted, axis=-1, keepdims=True) + NORM_EPS)
        unit = shifted * inv_std
        unit_ref[sl, :] = unit
        inv_ref[sl, :] = jnp.broadcast_to(inv_std, (256, 128))
        normed = (unit * gain_ref[...]).astype(BF16)
        qv = dot_nn(normed, win_ref[:, 0:D]) * scale
        q_ref[sl, :] = qv.astype(BF16)
        qt_ref[D * g : D * g + D, :] = qv.T.astype(BF16)
        kv = dot_nn(normed, win_ref[:, D : 2 * D])
        k_ref[sl, :] = kv.astype(BF16)
        kt_ref[D * g : D * g + D, :] = kv.T.astype(BF16)
        v_ref[sl, :] = dot_nn(normed, win_ref[:, 2 * D : 3 * D]).astype(BF16)
        if g == 0:
            fetch_out.wait()
        go = dot_nn(cot_ref[sl, :], wout_t_ref[...])
        go_ref[sl, :] = go.astype(BF16)
        got_ref[D * g : D * g + D, :] = go.T.astype(BF16)

    row = iota((16, 512), 0)
    ahead = (bits(iota((16, 512), 1), 0, 4) + row) < 16
    owner = lax.shift_right_logical(iota((256, 128), 1), 5)

    def only(rows, hh):
        pieces = [jnp.zeros((32 * hh, 256), BF16)] if hh else []
        pieces.append(rows)
        if hh < 3:
            pieces.append(jnp.zeros((96 - 32 * hh, 256), BF16))
        return jnp.concatenate(pieces, axis=0)

    def block(hb, carry):
        lanes = pl.ds(pl.multiple_of(hb * 128, 128), 128)

        def thin(g, hh):
            return pl.ds(pl.multiple_of(D * g + hb * 128 + 32 * hh, 32), 32)

        def forward(hh, g):
            sl = slice(256 * g, 256 * g + 256)
            scores = dot_nn(k_ref[sl, lanes], only(qt_ref[thin(g, hh), :], hh))
            grad_probs = dot_nn(v_ref[sl, lanes], only(got_ref[thin(g, hh), :], hh))
            return scores, grad_probs

        def soft(hh, scores, grad_probs, t):
            shifted = scores[:, t] + bias_ref[hh, :, t]
            exponent = jnp.exp(shifted - jnp.max(shifted, axis=0, keepdims=True))
            probs = exponent * (1.0 / jnp.sum(exponent, axis=0, keepdims=True))
            delta = jnp.sum(probs * grad_probs[:, t], axis=0, keepdims=True)
            grad = probs * (grad_probs[:, t] - delta)
            return probs.astype(BF16), grad.astype(BF16), grad

        def weigh_values(hh, g, probs_half):
            sl = slice(256 * g, 256 * g + 256)
            grad_v = dot_nn(probs_half, go_ref[sl, lanes])
            pltpu.store(dv_part.at[sl, :], grad_v, mask=owner == hh)

        def weigh_scores(hh, g, half):
            sl = slice(256 * g, 256 * g + 256)
            pltpu.store(dk_part.at[sl, :], dot_nn(half, q_ref[sl, lanes]), mask=owner == hh)
            dqt_ref[thin(g, hh), :] = dot_nn(kt_ref[thin(g, hh), :], half) * scale

        def fold_table(hh, left, right):
            fold = None
            blank = jnp.zeros((16, 128), F32)
            for r in range(8):
                a = slice(16 * (15 - r), 16 * (15 - r) + 16)
                b = slice(16 * (7 - r), 16 * (7 - r) + 16)
                wide = jnp.concatenate([left[a], right[a] + left[b], right[b], blank], axis=1)
                if r:
                    wide = pltpu.roll(wide, 16 * r, 1)
                fold = wide if fold is None else fold + wide
            for b in (1, 2, 4, 8):
                fold = jnp.where(lax.bitwise_and(row, b) != 0, pltpu.roll(fold, 512 - b, 1), fold)
            near = jnp.where(ahead, fold, 0.0)
            h = hb * 4 + hh
            pn_ref[pl.ds(h, 1), 0:512] = jnp.sum(near, axis=0, keepdims=True)
            pn_ref[pl.ds(h, 1), 512:1024] = jnp.sum(fold - near, axis=0, keepdims=True)

        def spread_bias(hh):
            line = line_ref[pl.ds(pl.multiple_of(64 * hb + 16 * hh, 16), 16), :]
            for r in range(8):
                turned = line if r == 0 else pltpu.roll(line, 512 - 16 * r, 1)
                bias_ref[hh, 16 * (15 - r) : 16 * (15 - r) + 16, :] = turned[:, 0:256]
                bias_ref[hh, 16 * (7 - r) : 16 * (7 - r) + 16, :] = turned[:, 128:384]

        units = [(hh, g) for hh in range(4) for g in range(2)]
        spread_bias(0)
        ready = forward(*units[0])
        total = late = None
        for n, (hh, g) in enumerate(units):
            after = forward(*units[n + 1]) if n + 1 < len(units) else None
            low = soft(hh, *ready, slice(0, 128))
            if late is not None:
                weigh_values(*late[0:3])
            if g == 0 and hh < 3:
                spread_bias(hh + 1)
            high = soft(hh, *ready, slice(128, 256))
            if late is not None:
                weigh_scores(*late[0:2], late[3])
            ready = after
            late = (
                hh,
                g,
                jnp.concatenate([low[0], high[0]], axis=1),
                jnp.concatenate([low[1], high[1]], axis=1),
            )
            if g == 0:
                total = low[2], high[2]
            else:
                fold_table(hh, total[0] + low[2], total[1] + high[2])
        weigh_values(*late[0:3])
        weigh_scores(*late[0:2], late[3])
        dk_ref[:, lanes] = dk_part[...].astype(BF16)
        dv_ref[:, lanes] = dv_part[...].astype(BF16)
        return carry

    fetch_lines.wait()
    lax.fori_loop(0, 4, block, 0)
    fetch_in.wait()

    for g in range(2):
        sl = slice(256 * g, 256 * g + 256)
        grad_q = dqt_ref[D * g : D * g + D, :].T.astype(BF16)
        grad_normed = (
            dot_nn(grad_q, win_t_ref[0:D, :])
            + dot_nn(dk_ref[sl, :], win_t_ref[D : 2 * D, :])
            + dot_nn(dv_ref[sl, :], win_t_ref[2 * D : 3 * D, :])
        )
        grad_unit = grad_normed * gain_ref[...]
        unit = unit_ref[sl, :]
        grad_rows = inv_ref[sl, 0:1] * (
            grad_unit
            - jnp.mean(grad_unit, axis=-1, keepdims=True)
            - unit * jnp.mean(grad_unit * unit, axis=-1, keepdims=True)
        )
        tok_ref[sl, :] = grad_rows.astype(BF16)

    give = one_hot(
        lambda o: bits(o, 1, 1) * 128 + bits(o, 2, 1) * 64 + bits(o, 3, 5) * 2 + bits(o, 0, 1)
    )
    for q in range(4):
        rows = jnp.concatenate(
            [
                tok_ref[256 * g + 64 * q : 256 * g + 64 * q + 64, 256 * half : 256 * half + 256]
                for g in range(2)
                for half in range(2)
            ],
            axis=0,
        )
        out_ref[256 * q : 256 * q + 256, :] = move_rows(give, rows)


def device_index(z, y, x, core):
    return (z * 4 + (y % 2) * 2 + core) * 8 + x * 2 + y // 2


def shift_pairs(turn, step):
    pairs = []
    for z in range(4):
        for y in range(4):
            for x in range(4):
                for core in range(2):
                    there = [z, x, y]
                    along = (turn + core) % 3
                    there[along] = (there[along] + step) % 4
                    pairs.append(
                        (
                            device_index(z, y, x, core),
                            device_index(there[0], there[2], there[1], core),
                        )
                    )
    return pairs


def other_core_pairs():
    return [(i, i ^ 8) for i in range(128)]


def sum_everywhere(part):
    core = lax.rem(lax.axis_index("ha"), 2)
    own = lax.dynamic_slice(part, (8 * core, 0), (8, 1024))
    given = lax.dynamic_slice(part, (8 * (1 - core), 0), (8, 1024))
    got = lax.ppermute(given, AXES, other_core_pairs())
    own = own + got
    for turn in range(3):
        one, two, three = (lax.ppermute(own, AXES, shift_pairs(turn, s)) for s in (1, 2, 3))
        own = (own + two) + (one + three)
    other = lax.ppermute(own, AXES, other_core_pairs())
    low = jnp.where(core == 0, own, other)
    high = jnp.where(core == 0, other, own)
    return jnp.concatenate([low, high], axis=0)


def split_bias(bias_table):
    zero = jnp.zeros((HEADS, 1, 16), F32)
    near = jnp.concatenate([bias_table[:, :, 15:31], zero], axis=1)
    far = jnp.pad(bias_table[:, :, 0:15], ((0, 0), (0, 0), (1, 0)))
    far = jnp.concatenate([far[:, 1:31], zero, far[:, 0:1]], axis=1)
    return near.reshape(HEADS, 512), far.reshape(HEADS, 512)


def join_table(part):
    by_row = part.reshape(HEADS, 2, 32, 16).transpose(2, 0, 1, 3)
    near = by_row[0:31, :, 0]
    far = jnp.concatenate([by_row[31:32, :, 1], by_row[0:30, :, 1]], axis=0)[:, :, 1:16]
    return jnp.concatenate([far, near], axis=2).transpose(1, 0, 2)


def vmem_specs(count):
    return [pl.BlockSpec(memory_space=pltpu.VMEM)] * count


def step(tokens, cotangent, norm_gain, in_weight, out_weight, bias_table):
    sent = pl.pallas_call(
        pack_kernel,
        out_shape=jax.ShapeDtypeStruct((1024, D), BF16),
        in_specs=[pl.BlockSpec(memory_space=pl.ANY)] * 2,
        out_specs=pl.BlockSpec(memory_space=pl.ANY),
        scratch_shapes=[
            pltpu.VMEM((4, 2, 4, 32, D), BF16),
            pltpu.VMEM((1024, D), BF16),
            pltpu.SemaphoreType.DMA((4, 2)),
            pltpu.SemaphoreType.DMA((4,)),
        ],
    )(tokens, cotangent)
    near, far = split_bias(bias_table)
    got = lax.all_to_all(sent.reshape(128, 8, D), AXES, split_axis=0, concat_axis=0, tiled=True)
    lines, turned = pl.pallas_call(
        prep_kernel,
        out_shape=(
            jax.ShapeDtypeStruct((LINE_ROWS, 512), F32),
            jax.ShapeDtypeStruct((4 * D, D), BF16),
        ),
        in_specs=vmem_specs(4),
        out_specs=(pl.BlockSpec(memory_space=pl.ANY), vmem_specs(1)[0]),
        scratch_shapes=[pltpu.VMEM((256, 512), F32), pltpu.SemaphoreType.DMA],
        compiler_params=pltpu.CompilerParams(vmem_limit_bytes=LARGE_GRANT),
    )(near, far, in_weight, out_weight)
    back, part = pl.pallas_call(
        group_kernel,
        out_shape=(
            jax.ShapeDtypeStruct((1024, 256), BF16),
            jax.ShapeDtypeStruct((HEADS, 1024), F32),
        ),
        in_specs=vmem_specs(3) + [pl.BlockSpec(memory_space=pltpu.HBM)] * 2,
        out_specs=tuple(vmem_specs(2)),
        scratch_shapes=[
            pltpu.VMEM((512, D), F32),
            pltpu.VMEM((512, 128), F32),
            pltpu.VMEM((512, D), BF16),
            pltpu.VMEM((512, D), BF16),
            pltpu.VMEM((512, D), BF16),
            pltpu.VMEM((512, D), BF16),
            pltpu.VMEM((2 * D, 256), BF16),
            pltpu.VMEM((2 * D, 256), BF16),
            pltpu.VMEM((2 * D, 256), BF16),
            pltpu.VMEM((2 * D, 256), F32),
            pltpu.VMEM((512, D), BF16),
            pltpu.VMEM((512, D), BF16),
            pltpu.VMEM((512, D), BF16),
            pltpu.VMEM((512, D), BF16),
            pltpu.VMEM((512, 128), F32),
            pltpu.VMEM((512, 128), F32),
            pltpu.VMEM((3 * D, D), BF16),
            pltpu.VMEM((D, D), BF16),
            pltpu.VMEM((4, 256, 256), F32),
            pltpu.VMEM((256, 512), F32),
            pltpu.SemaphoreType.DMA((3,)),
        ],
        compiler_params=pltpu.CompilerParams(vmem_limit_bytes=LARGE_GRANT),
        cost_estimate=pl.CostEstimate(
            flops=20_000_000_000, bytes_accessed=8_000_000, transcendentals=2_000_000
        ),
    )(got.reshape(1024, D), norm_gain.reshape(1, D), in_weight, lines, turned)
    returned = lax.all_to_all(
        back.reshape(128, 8, 256), AXES, split_axis=0, concat_axis=0, tiled=True
    )
    table = join_table(sum_everywhere(part))
    unpack = pl.pallas_call(
        unpack_kernel,
        out_shape=jax.ShapeDtypeStruct((16, 32, D), BF16),
        in_specs=vmem_specs(1),
        out_specs=vmem_specs(1)[0],
        compiler_params=pltpu.CompilerParams(vmem_limit_bytes=SMALL_GRANT),
    )
    grad_input = unpack(returned.reshape(1024, 256))
    return (grad_input, table)


def solution(mesh):
    in_specs = (P("ha", "wa", None), P("ha", "wa", None), P(), P(), P(), P())
    out_specs = (P("ha", "wa", None), P())
    return jax.shard_map(step, mesh=mesh, in_specs=in_specs, out_specs=out_specs, check_vma=False)
```
